32 devices in a mesh: fourier: 4 (over y, core), meridian: 8 (over z, x).
Axes of the slice: x: 2, y: 2, z: 4, core: 2. Of those that a mesh axis runs over, the one named last changes fastest.
Arguments:
- forward_now: float32 [3, 1056, 2048], P(None, 'meridian', 'fourier'), may hold values from -3 to 3
- forward_last: float32 [3, 1056, 2048], P(None, 'meridian', 'fourier'), may hold values from -3 to 3
- adjoint_now: float32 [3, 1056, 2048], P(None, 'meridian', 'fourier'), may hold values from -3 to 3
- adjoint_last: float32 [3, 1056, 2048], P(None, 'meridian', 'fourier'), may hold values from -3 to 3
- moduli: float32 [21, 17, 8, 400], P(None, None, 'meridian', 'fourier'), may hold values from -1.8 to 1.8
- inv_radius: float32 [3200], P('meridian'), may hold values from 0.0009765625 to 0.0078125
- inv_mass: float32 [2112], P('meridian'), may hold values from 0.005 to 0.05
Outputs:
- forward_next: float32 [3, 1056, 2048], P(None, 'meridian', 'fourier')
- adjoint_next: float32 [3, 1056, 2048], P(None, 'meridian', 'fourier')
- kernel: float32 [21, 17, 8, 400], P(None, None, 'meridian', 'fourier')
The draws below stay inside these ranges and needn't reach their ends.
All inputs are finite; a program needn't handle non-finite values.
Results may differ from the reference program's by a relative error of at most 0.0001.
Values sent between devices are 32-bit elements; how exact they have to be, the bound alone decides.
A program may use at most 128 MiB of HBM per device.

```python
import math
import jax
import jax.numpy as jnp
import numpy as np
from jax import lax

F = 1024
ORD = 8
EB = 8
EA = 2
BASIS = 17
SLICES = 8
NPTS = 2112
Q = 400
NQ = 3200
N_MERIDIAN = 8


def block_levels(stream_key, dims, pieces, least, top_value):
    loudness, own = 1.0, jax.random.fold_in(stream_key, 6)
    for axis_at, parts in pieces:
        draws = jnp.exp(jax.random.uniform(jax.random.fold_in(own, axis_at), (parts,), jnp.float32, least / len(pieces), top_value / len(pieces)))
        loudness = loudness * jnp.repeat(draws, dims[axis_at] // parts).reshape([-1 if axis == axis_at else 1 for axis in range(len(dims))])
    return loudness


def normal_values(own_key, shape, spread, reach, shards=(), kind=jnp.bfloat16):
    gain = block_levels(own_key, shape, shards, -0.22, 0.18) if shards else 1.0
    drawn = jax.random.normal(own_key, shape, jnp.float32) * spread * gain
    return jnp.minimum(jnp.maximum(drawn, -reach), reach).astype(kind)


def setup_inputs(seed: int = 0) -> dict:
    key_of = jax.random.split(jax.random.key(seed), 8)
    forward_now = normal_values(key_of[0], (3, NPTS // 2, 2 * F), 0.5, 3.0, ((1, 8), (2, 4)), jnp.float32)
    forward_last = normal_values(key_of[1], (3, NPTS // 2, 2 * F), 0.5, 3.0, ((1, 8), (2, 4)), jnp.float32)
    adjoint_now = normal_values(key_of[2], (3, NPTS // 2, 2 * F), 0.5, 3.0, ((1, 8), (2, 4)), jnp.float32)
    adjoint_last = normal_values(key_of[3], (3, NPTS // 2, 2 * F), 0.5, 3.0, ((1, 8), (2, 4)), jnp.float32)
    moduli = normal_values(key_of[4], (21, BASIS, SLICES, Q), 0.3, 1.8, ((2, 8), (3, 4)), jnp.float32)
    inv_radius = jnp.clip(jnp.exp(math.log(0.0078125) - 2.0794415 * jax.random.uniform(key_of[5], (NQ,), jnp.float32) ** block_levels(key_of[5], (NQ,), ((0, 8),), -0.2, 0.2)), 0.0009765625, 0.0078125)
    inv_mass = jnp.clip(jnp.exp(math.log(0.05) - 2.3025851 * jax.random.uniform(key_of[6], (NPTS,), jnp.float32) ** block_levels(key_of[6], (NPTS,), ((0, 8),), -0.2, 0.2)), 0.005, 0.05)
    return {"forward_now": forward_now, "forward_last": forward_last, "adjoint_now": adjoint_now, "adjoint_last": adjoint_last, "moduli": moduli, "inv_radius": inv_radius, "inv_mass": inv_mass}


highest = lax.Precision.HIGHEST
kernel_weight = 0.0001

def unpack_points(values):
    shape = values.shape
    evens = values[:, :, 0::2]
    odds = values[:, :, 1::2]
    return jnp.stack([evens, odds], axis=2).reshape(shape[0], 2 * shape[1], shape[2] // 2)

def pack_points(values):
    shape = values.shape
    paired = values.reshape(shape[0], shape[1] // 2, 2, shape[2])
    packed = jnp.zeros((shape[0], shape[1] // 2, 2 * shape[2]), values.dtype)
    packed = packed.at[:, :, 0::2].set(paired[:, :, 0])
    return packed.at[:, :, 1::2].set(paired[:, :, 1])

def gll_tables():
    points_x = np.array([-1.0, -math.sqrt(3.0 / 7.0), 0.0, math.sqrt(3.0 / 7.0), 1.0])
    weights = np.array([0.1, 49.0 / 90.0, 32.0 / 45.0, 49.0 / 90.0, 0.1])
    factor = np.array([np.prod([points_x[row_at] - points_x[column] for column in range(5) if column != row_at]) for row_at in range(5)])
    derive = np.zeros((5, 5))
    for row_at in range(5):
        for col_at in range(5):
            if row_at != col_at:
                derive[row_at, col_at] = factor[row_at] / (factor[col_at] * (points_x[row_at] - points_x[col_at]))
            else:
                derive[row_at, col_at] = sum((1.0 / (points_x[row_at] - points_x[column]) for column in range(5) if column != row_at))
    return (jnp.asarray(derive, jnp.float32), jnp.asarray(np.outer(weights, weights).reshape(25), jnp.float32))

def sample_table(count):
    sample_ids = jnp.arange(count, dtype=jnp.int32)
    orders = jnp.where(sample_ids == 1, count // 2, sample_ids // 2).astype(jnp.int32)
    phases = sample_ids[:, None] * orders[None, :] % count
    angles = phases.astype(jnp.float32) * (2.0 * math.pi / count)
    sine_cols = (sample_ids % 2 == 1) & (sample_ids != 1)
    return jnp.where(sine_cols[None, :], jnp.sin(angles), jnp.cos(angles))

def basis_table(count, degree):
    sample_ids = jnp.arange(count, dtype=jnp.int32)
    column = jnp.arange(2 * degree + 1, dtype=jnp.int32)
    orders = (column + 1) // 2
    phases = sample_ids[:, None] * orders[None, :] % count
    angles = phases.astype(jnp.float32) * (2.0 * math.pi / count)
    sine_cols = (column % 2 == 0) & (column > 0)
    return jnp.where(sine_cols[None, :], jnp.sin(angles), jnp.cos(angles))

def node_weights(weights, count):
    return jnp.tile(weights, count // 25)

def to_blocks(values, count):
    width = values.shape[-1]
    leading = values[..., :4 * count, :].reshape(values.shape[:-2] + (count, 4, width))
    closing = values[..., 4::4, :][..., None, :]
    return jnp.concatenate([leading, closing], axis=-2)

def from_blocks(blocks, count):
    width = blocks.shape[-1]
    outer = blocks.shape[:-3]
    edge_pad = [(0, 0)] * len(outer)
    leading = blocks[..., :4, :].reshape(outer + (4 * count, width))
    leading = jnp.pad(leading, edge_pad + [(0, 1), (0, 0)])
    closing = jnp.pad(blocks[..., 4:, :], edge_pad + [(0, 0), (3, 0), (0, 0)])
    closing = jnp.pad(closing.reshape(outer + (4 * count, width)), edge_pad + [(1, 0), (0, 0)])
    return leading + closing

def to_elements(field, count_a, count_b):
    leads = field.shape[0]
    width = field.shape[-1]
    columns = to_blocks(field, count_b)
    columns = jnp.transpose(columns, (0, 2, 3, 1, 4))
    grid_blocks = to_blocks(columns, count_a)
    grid_blocks = jnp.transpose(grid_blocks, (0, 3, 1, 4, 2, 5))
    return grid_blocks.reshape(leads, count_a * count_b, 5, 5, width)

def from_elements(elements, count_a, count_b):
    leads = elements.shape[0]
    width = elements.shape[-1]
    grid_blocks = elements.reshape(leads, count_a, count_b, 5, 5, width)
    grid_blocks = jnp.transpose(grid_blocks, (0, 2, 4, 1, 3, 5))
    row_sums = from_blocks(grid_blocks, count_a)
    row_sums = jnp.transpose(row_sums, (0, 3, 1, 2, 4))
    return from_blocks(row_sums, count_b)

def azimuth(values, orders):
    orders_each = jnp.repeat(orders, 2)
    positions = jnp.arange(values.shape[-1], dtype=jnp.int32)
    is_even = positions % 2 == 0
    following = jnp.roll(values, -1, axis=-1)
    preceding = jnp.roll(values, 1, axis=-1)
    return jnp.where(is_even, orders_each * following, -orders_each * preceding)

def strains(displace, radius, orders, derive):
    along_a = jnp.einsum('ik,lcekjn->lceijn', derive, displace, precision=highest)
    along_b = jnp.einsum('jk,lceikn->lceijn', derive, displace, precision=highest)
    beside_all = radius[..., None] * azimuth(displace, orders)
    return jnp.stack([along_a[:, 0], along_b[:, 1], beside_all[:, 2], along_b[:, 2] + beside_all[:, 1], along_a[:, 2] + beside_all[:, 0], along_a[:, 1] + along_b[:, 0]], axis=1)

def forces(stress, radius, orders, derive):
    part_a = jnp.stack([stress[:, 0], stress[:, 5], stress[:, 4]], axis=1)
    part_b = jnp.stack([stress[:, 5], stress[:, 1], stress[:, 3]], axis=1)
    part_p = jnp.stack([stress[:, 4], stress[:, 3], stress[:, 2]], axis=1)
    from_a = jnp.einsum('ki,lcekjn->lceijn', derive, part_a, precision=highest)
    from_b = jnp.einsum('kj,lceikn->lceijn', derive, part_b, precision=highest)
    return from_a + from_b - azimuth(radius[..., None] * part_p, orders)

def voigt_index(left_at, right_at):
    lesser = min(left_at, right_at)
    larger = max(left_at, right_at)
    return lesser * 6 - lesser * (lesser - 1) // 2 + larger - lesser

def stress_samples(strain, moduli_s, dft_table, weights_q):
    sampled = jnp.dot(strain, dft_table.T, precision=highest)
    stress_list = []
    for left_at in range(6):
        total = moduli_s[voigt_index(left_at, 0)] * sampled[:, 0]
        for right_at in range(1, 6):
            total = total + moduli_s[voigt_index(left_at, right_at)] * sampled[:, right_at]
        stress_list.append(total)
    weighted = jnp.stack(stress_list, axis=1) * weights_q[:, None]
    coeffs = jnp.dot(weighted, dft_table, precision=highest) / dft_table.shape[0]
    return (coeffs, sampled)

def kernel_terms(sampled, basis_rows, weights_q):
    forward_s = sampled[0]
    adjoint_s = sampled[1]
    terms = []
    for left_at in range(6):
        for right_at in range(left_at, 6):
            if left_at == right_at:
                terms.append(forward_s[left_at] * adjoint_s[left_at])
            else:
                terms.append(forward_s[left_at] * adjoint_s[right_at] + forward_s[right_at] * adjoint_s[left_at])
    stacked = jnp.stack(terms) * weights_q[:, None]
    projected = jnp.dot(stacked, basis_rows, precision=highest)
    return jnp.transpose(projected, (0, 2, 1)) * kernel_weight

def reference(forward_now, forward_last, adjoint_now, adjoint_last, moduli, inv_radius, inv_mass):
    forward_now = unpack_points(forward_now)
    forward_last = unpack_points(forward_last)
    adjoint_now = unpack_points(adjoint_now)
    adjoint_last = unpack_points(adjoint_last)
    derive, weights = gll_tables()
    width_b = 4 * EB + 1
    row_count = 4 * EA
    nodes_slice = 25 * EA * EB
    fields = jnp.stack([forward_now, adjoint_now]).reshape(2, 3, row_count * N_MERIDIAN, width_b, F)
    padded = jnp.pad(fields, ((0, 0), (0, 0), (0, 1), (0, 0), (0, 0)))
    dft_table = sample_table(F)
    basis_rows = basis_table(F, ORD)
    orders_full = jnp.arange(F // 2, dtype=jnp.int32).astype(jnp.float32)
    weights_q = node_weights(weights, nodes_slice)

    def one_slice(slice_at):
        block = lax.dynamic_slice_in_dim(padded, slice_at * row_count, row_count + 1, axis=2)
        block = block.reshape(6, row_count + 1, width_b, F)
        elements = to_elements(block, EA, EB).reshape(2, 3, EA * EB, 5, 5, F)
        radius = lax.dynamic_slice_in_dim(inv_radius, slice_at * nodes_slice, nodes_slice).reshape(EA * EB, 5, 5)
        moduli_m = lax.dynamic_index_in_dim(moduli, slice_at, axis=2, keepdims=False)
        moduli_s = jnp.einsum('cjq,nj->cqn', moduli_m, basis_rows, precision=highest)
        strain = strains(elements, radius, orders_full, derive).reshape(2, 6, nodes_slice, F)
        coeffs, sampled = stress_samples(strain, moduli_s, dft_table, weights_q)
        pushed = forces(coeffs.reshape(2, 6, EA * EB, 5, 5, F), radius, orders_full, derive)
        assembled = from_elements(pushed.reshape(6, EA * EB, 5, 5, F), EA, EB)
        return (assembled, kernel_terms(sampled, basis_rows, weights_q))
    assembled, kernel = lax.map(one_slice, jnp.arange(N_MERIDIAN, dtype=jnp.int32))
    own_rows = assembled[:, :, :row_count]
    carried = jnp.concatenate([jnp.zeros_like(assembled[:1, :, row_count]), assembled[:-1, :, row_count]], axis=0)
    own_rows = own_rows.at[:, :, 0].add(carried)
    forces_all = jnp.transpose(own_rows, (1, 0, 2, 3, 4)).reshape(2, 3, NPTS, F)
    mass_scale = inv_mass[:, None]
    forward_next = 2.0 * forward_now - forward_last - mass_scale * forces_all[0]
    adjoint_next = 2.0 * adjoint_now - adjoint_last - mass_scale * forces_all[1]
    return (pack_points(forward_next), pack_points(adjoint_next), jnp.transpose(kernel, (1, 2, 0, 3)))
```

```python
import functools
import math

import jax
import jax.numpy as jnp
import numpy as np
from jax import lax
from jax.experimental import pallas as pl
from jax.experimental.pallas import tpu as pltpu
from jax.sharding import PartitionSpec as P

ORD = 8
EB = 8
LANES = 128
kernel_weight = 0.0001
high = lax.Precision.HIGH
bf16 = jnp.bfloat16
f32 = jnp.float32
PAIRS = [(a, b) for a in range(6) for b in range(a, 6)]
PART_A, PART_B, PART_P = (0, 5, 4), (5, 1, 3), (4, 3, 2)


def gll_tables():
    x = np.array([-1.0, -math.sqrt(3.0 / 7.0), 0.0, math.sqrt(3.0 / 7.0), 1.0])
    weights = np.array([0.1, 49.0 / 90.0, 32.0 / 45.0, 49.0 / 90.0, 0.1])
    factor = np.array([np.prod([x[i] - x[k] for k in range(5) if k != i]) for i in range(5)])
    derive = np.zeros((5, 5))
    for i in range(5):
        for k in range(5):
            if i != k:
                derive[i, k] = factor[i] / (factor[k] * (x[i] - x[k]))
            else:
                derive[i, k] = sum(1.0 / (x[i] - x[o]) for o in range(5) if o != i)
    return derive, np.outer(weights, weights).reshape(25)


def split_host(values):
    wide = np.asarray(values, np.float32)
    hi = wide.astype(bf16)
    return hi, (wide - hi.astype(np.float32)).astype(bf16)


def split_device(values):
    hi = lax.reduce_precision(values, 8, 7)
    return hi.astype(bf16), (values - hi).astype(bf16)


def split_kernel(values):
    hi = values.astype(bf16)
    return hi, (values - hi.astype(f32)).astype(bf16)


def cosine_turn(phase, count):
    folded = (phase + count // 2) % count - count // 2
    x = (count // 4 - jnp.abs(folded)).astype(f32) * (2.0 * math.pi / count)
    y = x * x
    tail = 1.0 / 362880 - y * (1.0 / 39916800)
    return x * (1.0 + y * (-1.0 / 6 + y * (1.0 / 120 + y * (-1.0 / 5040 + y * tail))))


def sample_tables(count):
    n = lax.broadcasted_iota(jnp.int32, (count, count), 0)
    k = lax.broadcasted_iota(jnp.int32, (count, count), 1)
    pair = k // 2
    order = jnp.where(k == 1, count // 2, pair)
    odd = k % 2
    base = cosine_turn(n * order - jnp.where(k == 1, 0, odd * (count // 4)), count)
    turned = pair.astype(f32) * cosine_turn(n * pair + (1 - odd) * (count // 4), count)
    return base, turned


def basis_rows(count):
    n = lax.broadcasted_iota(jnp.int32, (count, 2 * ORD + 1), 0)
    j = lax.broadcasted_iota(jnp.int32, (count, 2 * ORD + 1), 1)
    sine = jnp.where((j % 2 == 0) & (j > 0), count // 4, 0)
    return cosine_turn(n * ((j + 1) // 2) - sine, count)


def nt(a, b):
    return lax.dot_general(a, b, (((1,), (1,)), ((), ())), preferred_element_type=f32)


def nn(a, b):
    return lax.dot_general(a, b, (((1,), (0,)), ((), ())), preferred_element_type=f32)


def dot3(left, right, op):
    return op(left[0], right[0]) + op(left[0], right[1]) + op(left[1], right[0])


def core(nf, pts, nodes, u_ref, bh_ref, bl_ref, zh_ref, zl_ref, am_ref, m_ref, gh_ref, gl_ref,
         rh_ref, rl_ref, gth_ref, gtl_ref, rth_ref, rtl_ref, out_ref, acc_ref,
         uh, ul, us, zs, cs, es, ss, ps, xs, ys):
    step = pl.program_id(0)
    local = u_ref.shape[2]

    @pl.when(step == 0)
    def _():
        for f in range(nf):
            hi, lo = split_kernel(u_ref[f])
            uh[:, f * local:(f + 1) * local] = hi
            ul[:, f * local:(f + 1) * local] = lo
        out_ref[...] = jnp.zeros_like(out_ref)
        acc_ref[...] = jnp.zeros_like(acc_ref)

    us[...] = nt(uh[...], bh_ref[...])
    us[...] += nt(uh[...], bl_ref[...])
    us[...] += nt(ul[...], bh_ref[...])
    zs[...] = nt(uh[...], zh_ref[...])
    zs[...] += nt(uh[...], zl_ref[...])
    zs[...] += nt(ul[...], zh_ref[...])
    cs[...] = nt(m_ref[...], am_ref[...])
    grads = (gh_ref[...], gl_ref[...])
    spins = (rh_ref[...], rl_ref[...])
    for l in range(2):
        ga, gb, gp = [], [], []
        for c in range(3):
            at = pl.ds((3 * l + c) * pts, pts)
            both = dot3(grads, split_kernel(us[at, :]), nn)
            ga.append(both[:nodes])
            gb.append(both[nodes:])
            gp.append(dot3(spins, split_kernel(zs[at, :]), nn))
        es[6 * l + 0] = ga[0]
        es[6 * l + 1] = gb[1]
        es[6 * l + 2] = gp[2]
        es[6 * l + 3] = gb[2] + gp[1]
        es[6 * l + 4] = ga[2] + gp[0]
        es[6 * l + 5] = ga[1] + gb[0]

    def tile(t, carry):
        row = pl.multiple_of(t * 8, 8)
        at = pl.ds(row, 8)
        fw = [es[v, at, :] for v in range(6)]
        ad = [es[6 + v, at, :] for v in range(6)]
        sf, sa = [None] * 6, [None] * 6

        def add(sums, v, term):
            sums[v] = term if sums[v] is None else sums[v] + term

        for r, (v, w) in enumerate(PAIRS):
            c = cs[pl.ds(pl.multiple_of(r * nodes + row, 8), 8), :]
            add(sf, v, c * fw[w])
            add(sa, v, c * ad[w])
            if v != w:
                add(sf, w, c * fw[v])
                add(sa, w, c * ad[v])
                prod = fw[v] * ad[w] + fw[w] * ad[v]
            else:
                prod = fw[v] * ad[v]
            ps[pl.ds(pl.multiple_of(r * nodes + row, 8), 8), :] = prod
        for v in range(6):
            ss[v, at, :] = sf[v]
            ss[6 + v, at, :] = sa[v]
        return carry

    lax.fori_loop(0, nodes // 8, tile, 0)
    ph, plo = split_kernel(ps[...])
    acc_ref[...] += nn(ph, am_ref[...]) + nn(plo, am_ref[...])
    gt = (gth_ref[...], gtl_ref[...])
    rt = (rth_ref[...], rtl_ref[...])
    for l in range(2):
        for c in range(3):
            at = pl.ds((3 * l + c) * pts, pts)
            ta, tb, tp = (6 * l + part[c] for part in (PART_A, PART_B, PART_P))
            pair = jnp.concatenate([ss[ta], ss[tb]], axis=0)
            xs[at, :] = dot3(gt, split_kernel(pair), nn)
            ys[at, :] = dot3(rt, split_kernel(ss[tp]), nn)
    xh, xl = split_kernel(xs[...])
    yh, yl = split_kernel(ys[...])
    for f in range(nf):
        cols = slice(f * local, (f + 1) * local)
        bh, zh = bh_ref[:, cols], zh_ref[:, cols]
        out_ref[f] += (nn(xh, bh) + nn(xl, bh) + nn(xh, bl_ref[:, cols])
                       + nn(yh, zh) + nn(yl, zh) + nn(yh, zl_ref[:, cols]))


def body(forward_now, forward_last, adjoint_now, adjoint_last, moduli, inv_radius, inv_mass):
    derive, weights = gll_tables()
    wide = 4 * EB + 1
    nf = lax.axis_size("fourier")
    nm = lax.axis_size("meridian")
    comps, rows, lanes = forward_now.shape
    local = lanes // 2
    total = local * nf
    row_count = 2 * rows // wide
    count_a = row_count // 4
    nodes_mine = moduli.shape[3]
    elements = nodes_mine // 25
    tile_b = min(elements, EB)
    tile_a = elements // tile_b
    points = (4 * tile_a + 1) * (4 * tile_b + 1)
    pts = -(-points // 16) * 16 if points % 16 > 8 or points % 16 == 0 else points // 16 * 16 + 8
    nodes = -(-nodes_mine // 8) * 8
    edge = (wide + 1) // 2

    pick = np.zeros((2, nf * pts, rows + edge), np.float32)
    for d in range(nf):
        ea, eb = d * elements // EB, d * elements % EB
        for i in range(4 * tile_a + 1):
            for j in range(4 * tile_b + 1):
                p = (4 * ea + i) * wide + 4 * eb + j
                pick[p % 2, d * pts + i * (4 * tile_b + 1) + j, p // 2] = 1.0
    pick = [jnp.asarray(part.astype(bf16)).astype(f32) for part in pick]
    grads = np.zeros((2, nodes, pts))
    node_at = np.zeros((nodes, pts))
    for ea in range(tile_a):
        for eb in range(tile_b):
            for i in range(5):
                for j in range(5):
                    q = ((ea * tile_b + eb) * 5 + i) * 5 + j
                    at = lambda a, b: (4 * ea + a) * (4 * tile_b + 1) + 4 * eb + b
                    node_at[q, at(i, j)] = 1.0
                    for k in range(5):
                        grads[0, q, at(k, j)] += derive[i, k]
                        grads[1, q, at(i, k)] += derive[j, k]
    grads = grads.reshape(2 * nodes, pts)
    gh, gl = (jnp.asarray(part) for part in split_host(grads))
    gth, gtl = (jnp.asarray(part) for part in split_host(grads.T))
    start = lax.axis_index("fourier") * nodes_mine
    radius = lax.dynamic_slice_in_dim(inv_radius, start, nodes_mine)
    radius = jnp.pad(radius, (0, nodes - nodes_mine))
    spin = jnp.asarray(node_at, f32) * radius[:, None]
    spin_t = jnp.asarray(node_at.T, f32) * radius[None, :]
    rh, rl = split_device(spin)
    rth, rtl = split_device(spin_t)

    lane = lax.broadcasted_iota(jnp.int32, (lanes, lanes), 0)
    spot = lax.broadcasted_iota(jnp.int32, (lanes, lanes), 1)
    order = ((lane % 2) * local + lane // 2 == spot).astype(f32)

    packed = jnp.concatenate([forward_now, adjoint_now], axis=0)
    below = [(i + 1, i) for i in range(nm - 1)]
    above = [(i, i + 1) for i in range(nm - 1)]
    upper = lax.ppermute(packed[:, :edge], "meridian", below)
    packed = jnp.concatenate([packed, upper], axis=1)
    apart = jnp.einsum("crx,xy->cry", packed, order, precision=high)
    tiles = (jnp.einsum("sr,crk->sck", pick[0], apart[:, :, :local], precision=high)
             + jnp.einsum("sr,crk->sck", pick[1], apart[:, :, local:], precision=high))
    tiles = jnp.transpose(tiles.reshape(nf, pts, 2 * comps, local), (0, 2, 1, 3))
    tiles = tiles.reshape(nf, 2 * comps * pts, local)
    mine = lax.all_to_all(tiles, "fourier", split_axis=0, concat_axis=0, tiled=True)

    base, turned = sample_tables(total)
    bh, bl = split_device(base)
    zh, zl = split_device(turned)
    ah, al = split_device(basis_rows(total))
    basis = 2 * ORD + 1
    am = jnp.pad(jnp.concatenate([ah, al, ah], axis=1), ((0, 0), (0, LANES - 3 * basis)))
    wq = jnp.asarray(np.tile(weights, elements), f32)
    scaled = jnp.transpose(moduli[:, :, 0, :] * (wq / total), (0, 2, 1))
    mh, ml = split_device(jnp.pad(scaled, ((0, 0), (0, nodes - nodes_mine), (0, 0))))
    m3 = jnp.concatenate([mh, mh, ml], axis=2)
    m3 = jnp.pad(m3, ((0, 0), (0, 0), (0, LANES - 3 * basis))).reshape(21 * nodes, LANES)

    chunk = min(256, total)
    width = 2 * comps * pts
    whole = lambda shape: pl.BlockSpec(shape, lambda i: (0,) * len(shape))
    table = pl.BlockSpec((chunk, total), lambda i: (i, 0))
    pushed, acc = pl.pallas_call(
        functools.partial(core, nf, pts, nodes),
        grid=(total // chunk,),
        out_shape=(jax.ShapeDtypeStruct((nf, width, local), f32),
                   jax.ShapeDtypeStruct((21 * nodes, LANES), f32)),
        in_specs=[whole((nf, width, local)), table, table, table, table,
                  pl.BlockSpec((chunk, LANES), lambda i: (i, 0)), whole((21 * nodes, LANES)),
                  whole(gh.shape), whole(gh.shape), whole(rh.shape), whole(rh.shape),
                  whole(gth.shape), whole(gth.shape), whole(rth.shape), whole(rth.shape)],
        out_specs=(whole((nf, width, local)), whole((21 * nodes, LANES))),
        scratch_shapes=[pltpu.VMEM((width, total), bf16), pltpu.VMEM((width, total), bf16),
                        pltpu.VMEM((width, chunk), f32), pltpu.VMEM((width, chunk), f32),
                        pltpu.VMEM((21 * nodes, chunk), f32),
                        pltpu.VMEM((12, nodes, chunk), f32), pltpu.VMEM((12, nodes, chunk), f32),
                        pltpu.VMEM((21 * nodes, chunk), f32),
                        pltpu.VMEM((width, chunk), f32), pltpu.VMEM((width, chunk), f32)],
        compiler_params=pltpu.CompilerParams(dimension_semantics=("arbitrary",),
                                             vmem_limit_bytes=56 * 1024 * 1024),
        cost_estimate=pl.CostEstimate(flops=24 * width * total * total, transcendentals=0,
                                      bytes_accessed=8 * total * total + 8 * width * total),
    )(mine, bh, bl, zh, zl, am, m3, gh, gl, rh, rl, gth, gtl, rth, rtl)

    back = lax.all_to_all(pushed, "fourier", split_axis=0, concat_axis=0, tiled=True)
    back = back.reshape(nf, 2 * comps, pts, local)
    sums = [jnp.einsum("dpr,dcpk->crk", part.reshape(nf, pts, rows + edge), back, precision=high)
            for part in pick]
    force = (jnp.einsum("crk,xk->crx", sums[0], order[:, :local], precision=high)
             + jnp.einsum("crk,xk->crx", sums[1], order[:, local:], precision=high))
    carried = lax.ppermute(force[:, rows:], "meridian", above)
    force = force[:, :rows] + jnp.pad(carried, ((0, 0), (0, rows - edge), (0, 0)))
    mass = inv_mass.reshape(rows, 2)
    is_even = lax.broadcasted_iota(jnp.int32, (rows, lanes), 1) % 2 == 0
    mass = jnp.where(is_even, mass[:, :1], mass[:, 1:])
    forward_next = 2.0 * forward_now - forward_last - mass * force[:comps]
    adjoint_next = 2.0 * adjoint_now - adjoint_last - mass * force[comps:]
    acc = acc.reshape(21, nodes, LANES)[:, :nodes_mine]
    terms = (acc[:, :, :basis] + acc[:, :, basis:2 * basis]) * (wq * kernel_weight)[:, None]
    return (forward_next, adjoint_next, jnp.transpose(terms, (0, 2, 1))[:, :, None, :])


def solution(mesh):
    field = P(None, "meridian", "fourier")
    grid = P(None, None, "meridian", "fourier")
    in_specs = (field, field, field, field, grid, P("meridian"), P("meridian"))
    return jax.shard_map(body, mesh=mesh, in_specs=in_specs, out_specs=(field, field, grid),
                         check_vma=False)
```
